128 devices in a mesh: row: 16 (over y, x_lo, core), col: 8 (over z, x_hi).
Axes of the slice: x: 4 (x_hi: 2, x_lo: 2; x = x_hi * 2 + x_lo), y: 4, z: 4, core: 2. Of those that a mesh axis runs over, the one named last changes fastest.
Arguments:
- activations: bfloat16 [1024, 64, 5120], P(('row', 'col')), may hold values from -6 to 6
- out_grads: bfloat16 [1024, 64, 8192], P(('row', 'col')), may hold values from -6 to 6
- lengths: int32 [1024], P(('row', 'col')), may hold values from 16 to 64
- proj_in: bfloat16 [5120, 128], replicated, may hold values from -0.078125 to 0.078125
- proj_out: bfloat16 [8192, 128], replicated, may hold values from -0.0625 to 0.0625
Outputs:
- fisher: float32 [16384, 16384], P('row', 'col')
The draws below stay inside these ranges and needn't reach their ends.
All inputs are finite; a program needn't handle non-finite values.
Results may differ from the reference program's by a relative error of at most 0.0068.
Values may be sent and summed in bfloat16 or wider, within the bound.
No kernel may reach another device: no remote copies, remote signals or barrier semaphores. Data moves between devices by JAX's collectives and lax.ppermute only.
A program may use at most 128 MiB of HBM per device.

```python
import jax
import jax.numpy as jnp

D = 5120
Q = 8192
RANK = 128
L = 64
EXAMPLES = 1024
ORDER = 16384


def touch_ends(array, stream_key, low, largest):
    longest = array.shape.index(max(array.shape))
    spots = []
    for shift in (0, 1):
        where = [jax.random.randint(jax.random.fold_in(stream_key, axis), (), 0, length) for axis, length in enumerate(array.shape)]
        where[longest] = (where[longest] + shift) % array.shape[longest]
        spots.append(tuple(where))
    return array.at[spots[0]].set(low).at[spots[1]].set(largest)


def block_levels(rng, extent, shards, least, top_value):
    gain = 1.0
    for dim, shards_of in shards:
        heights = jax.random.uniform(jax.random.fold_in(jax.random.fold_in(rng, 6), dim), (shards_of,), jnp.float32, least / len(shards), top_value / len(shards))
        gain = gain * jnp.repeat(jnp.exp(heights), extent[dim] // shards_of).reshape((-1,) + (1,) * (len(extent) - 1 - dim))
    return gain


def bell_draw(own_key, shape, width, most, pieces=(), kind=jnp.bfloat16):
    values = jax.random.normal(own_key, shape, jnp.float32) * width
    if len(pieces) > 0:
        values = block_levels(own_key, shape, pieces, -0.22, 0.18) * values
    return jnp.clip(values, min=-most, max=most).astype(kind)


def setup_inputs(seed: int = 0) -> dict:
    seeds = jax.random.split(jax.random.key(seed), 6)
    activations = bell_draw(seeds[0], (EXAMPLES, L, D), 1.0, 6.0, ((0, 128),))
    out_grads = bell_draw(seeds[1], (EXAMPLES, L, Q), 1.0, 6.0, ((0, 128),))
    lengths = touch_ends(jax.random.randint(seeds[2], (EXAMPLES,), L // 4, L + 1), jax.random.fold_in(seeds[2], 1), L // 4, L).astype(jnp.int32)
    proj_in = bell_draw(seeds[3], (D, RANK), D ** -0.5, 0.078125)
    proj_out = bell_draw(seeds[4], (Q, RANK), Q ** -0.5, 0.0625)
    return dict(activations=activations, out_grads=out_grads, lengths=lengths, proj_in=proj_in, proj_out=proj_out)


def reference(activations, out_grads, lengths, proj_in, proj_out):
    in_factors = jnp.einsum('etd,dr->etr', activations.astype(jnp.float32), proj_in.astype(jnp.float32)).astype(jnp.bfloat16)
    out_raw = jnp.einsum('etq,qr->etr', out_grads.astype(jnp.float32), proj_out.astype(jnp.float32))
    positions = jnp.arange(L, dtype=jnp.int32)
    valid = (positions[None, :] < lengths[:, None]).astype(jnp.float32)
    out_factors = (out_raw * valid[:, :, None]).astype(jnp.bfloat16)
    grads = jnp.einsum('eti,etj->eij', out_factors.astype(jnp.float32), in_factors.astype(jnp.float32))
    grads = (grads * (1.0 / jnp.sqrt(jnp.float32(L)))).astype(jnp.bfloat16).reshape(EXAMPLES, ORDER)
    wide = grads.astype(jnp.float32)
    fisher = jnp.dot(wide.T, wide) * (1.0 / jnp.sqrt(jnp.float32(EXAMPLES)))
    return fisher
```

```python
import functools

import jax
import jax.numpy as jnp
from jax import lax
from jax.experimental import pallas as pl
from jax.experimental.pallas import tpu as pltpu
from jax.sharding import PartitionSpec as P

L = 64
AXES = ("row", "col")
SIZE = {"core": 2, "x_lo": 2, "y": 4, "x_hi": 2, "z": 4}


def decode(row, col):
    return {"core": row % 2, "x_lo": (row // 2) % 2, "y": row // 4, "x_hi": col % 2, "z": col // 2}


def encode(place):
    return (place["y"] * 2 + place["x_lo"]) * 2 + place["core"], place["z"] * 2 + place["x_hi"]


def permute(name, value, move):
    n_row, n_col = lax.axis_size("row"), lax.axis_size("col")
    pairs = []
    for row in range(n_row):
        for col in range(n_col):
            to_row, to_col = encode(move(decode(row, col)))
            pairs.append((row * n_col + col, to_row * n_col + to_col))
    with jax.named_scope(name):
        return lax.ppermute(value, AXES, pairs)


def fetch(name, value, **steps):
    def move(place):
        return {axis: (at - steps.get(axis, 0)) % SIZE[axis] for axis, at in place.items()}

    return permute(name, value, move)


def swap(place):
    return {
        "core": place["core"],
        "x_lo": place["x_hi"],
        "y": (place["y"] + place["z"]) % 4,
        "x_hi": place["x_lo"],
        "z": place["y"],
    }


def fisher_kernel(scale, where, *refs):
    lefts, rights, others = refs[0:8], refs[8:16], refs[16:24]
    out, left_buf, right_buf, sems = refs[24:]
    half, tile = pl.program_id(0), pl.program_id(1)
    turn, flip = where[1], where[2]
    depth = lefts[0].shape[0]

    def left_copy(i):
        slot = ((i // 2 - turn + 4) % 4) * 2 + jnp.bitwise_xor(i % 2, flip)
        to = left_buf.at[pl.ds(pl.multiple_of(slot * depth, depth), depth)]
        return pltpu.make_async_copy(lefts[i], to, sems.at[i])

    def right_copy(which, i):
        source = (rights, others)[which][i]
        to = right_buf.at[which, pl.ds(i * depth, depth)]
        return pltpu.make_async_copy(source, to, sems.at[8 + which * 8 + i])

    @pl.when(jnp.logical_and(half == 0, tile == 0))
    def _():
        for i in range(8):
            left_copy(i).start()
            right_copy(0, i).start()
        for i in range(8):
            right_copy(1, i).start()
        for i in range(8):
            left_copy(i).wait()
            right_copy(0, i).wait()

    @pl.when(jnp.logical_and(half == 1, tile == 0))
    def _():
        for i in range(8):
            right_copy(1, i).wait()

    wide = out.shape[0]
    part = left_buf[:, pl.ds(pl.multiple_of(tile * wide, wide), wide)]
    out[...] = scale * lax.dot_general(
        part, right_buf[half], (((0,), (0,)), ((), ())), preferred_element_type=jnp.float32
    )


def fisher_block(where, lefts, rights, others, scale):
    depth, width = lefts[0].shape
    total = depth * 8
    tiles = 4
    return pl.pallas_call(
        functools.partial(fisher_kernel, scale),
        grid_spec=pltpu.PrefetchScalarGridSpec(
            num_scalar_prefetch=1,
            grid=(2, tiles),
            in_specs=[pl.BlockSpec(memory_space=pl.ANY)] * 24,
            out_specs=pl.BlockSpec(
                (width // tiles, width), lambda h, t, where: (t, jnp.bitwise_xor(h, where[0]))
            ),
            scratch_shapes=[
                pltpu.VMEM((total, width), jnp.bfloat16),
                pltpu.VMEM((2, total, width), jnp.bfloat16),
                pltpu.SemaphoreType.DMA((24,)),
            ],
        ),
        out_shape=jax.ShapeDtypeStruct((width, 2 * width), jnp.float32),
        compiler_params=pltpu.CompilerParams(vmem_limit_bytes=40 * 1024 * 1024),
        cost_estimate=pl.CostEstimate(
            flops=4 * total * width * width,
            bytes_accessed=6 * total * width + 8 * width * width,
            transcendentals=0,
        ),
        name="fisher_block",
    )(where, *lefts, *rights, *others)


def on_device(activations, out_grads, lengths, proj_in, proj_out):
    local_ex = activations.shape[0]
    width = proj_in.shape[1]
    order = width * width
    in_factors = jnp.dot(
        activations.reshape(local_ex * L, -1), proj_in, preferred_element_type=jnp.float32
    ).astype(jnp.bfloat16)
    out_raw = jnp.dot(
        out_grads.reshape(local_ex * L, -1), proj_out, preferred_element_type=jnp.float32
    )
    positions = lax.broadcasted_iota(jnp.int32, (local_ex, L), 1)
    valid = (positions < lengths[:, None]).astype(jnp.float32).reshape(local_ex * L, 1)
    out_factors = (out_raw * valid).astype(jnp.bfloat16)
    grads = jnp.einsum(
        "eti,etj->eij",
        out_factors.reshape(local_ex, L, width),
        in_factors.reshape(local_ex, L, width),
        preferred_element_type=jnp.float32,
    )
    n_row = lax.axis_size("row")
    n_col = lax.axis_size("col")
    row_width = order // n_row
    total_ex = local_ex * n_row * n_col
    grads = (grads * (1.0 / jnp.sqrt(jnp.float32(L)))).astype(jnp.bfloat16)
    grads = grads.reshape(local_ex, n_row, row_width).transpose(1, 0, 2)
    mine = lax.all_to_all(grads, "row", 0, 0, tiled=True).reshape(local_ex * n_row, row_width)

    r = permute("swap", mine, swap)
    lx = fetch("l_x", mine, x_hi=1)
    lz1 = fetch("l_z1", mine, z=1)
    lz3 = fetch("l_z3", mine, z=3)
    lz2 = fetch("l_z2", mine, z=2)
    lxz1 = fetch("l_xz1", lx, z=1)
    lxz3 = fetch("l_xz3", lx, z=3)
    lxz2 = fetch("l_xz2", lz2, x_hi=1)
    rx = fetch("r_x", r, x_lo=1)
    ry1 = fetch("r_y1", r, y=1)
    ry3 = fetch("r_y3", r, y=3)
    ry2 = fetch("r_y2", r, y=2)
    rxy1 = fetch("r_xy1", rx, y=1)
    rxy3 = fetch("r_xy3", rx, y=3)
    rxy2 = fetch("r_xy2", ry2, x_lo=1)
    lefts = [mine, lx, lz1, lxz1, lz2, lxz2, lz3, lxz3]
    rights = [r, rx, ry1, rxy1, ry2, rxy2, ry3, rxy3]
    others = [fetch(f"o_{i}", piece, core=1) for i, piece in enumerate(rights)]

    row, col = lax.axis_index("row"), lax.axis_index("col")
    core, x_lo, y = row % 2, (row // 2) % 2, row // 4
    x_hi, z = col % 2, col // 2
    where = jnp.stack([core, (y - 2 * z) % 4, jnp.bitwise_xor(x_lo, x_hi)]).astype(jnp.int32)
    return fisher_block(where, lefts, rights, others, float(total_ex) ** -0.5)


def solution(mesh):
    placed = (
        P(("row", "col"), None, None),
        P(("row", "col"), None, None),
        P(("row", "col")),
        P(),
        P(),
    )
    return jax.shard_map(
        on_device, mesh=mesh, in_specs=placed, out_specs=P("row", "col"), check_vma=False
    )
```
